32 devices in a mesh: parts: 2 (over x), outer: 8 (over z, y), inner: 2 (over core).
Axes of the slice: x: 2, y: 2, z: 4, core: 2. Of those that a mesh axis runs over, the one named last changes fastest.
Arguments:
- queries: bfloat16 [8192, 1024], P(('parts', 'outer', 'inner')), parts along dimension 0, may hold values from -72 to 72
- key_rows: bfloat16 [8192, 128], P(('parts', 'outer', 'inner')), parts along dimension 0, may hold values from -6 to 6
- value_rows: bfloat16 [8192, 128], P(('parts', 'outer', 'inner')), parts along dimension 0, may hold values from -6 to 6
- vertical: int32 [16, 8], P('parts'), parts along dimension 0, may hold values from 0 to 63, as said below
- slash_offsets: int32 [16, 8], P('parts'), parts along dimension 0, may hold values from 0 to 63, as said below
Outputs:
- attended: bfloat16 [8192, 1024], P(('parts', 'outer', 'inner')), parts along dimension 0
The draws below stay inside these ranges and needn't reach their ends.
There are 2 independent parts, one for each index of `parts`. The reference program is written for one: setup_inputs(seed, part) draws one part's arguments, and reference() takes and returns one part's arrays. A program takes and returns all parts, laid end to end along the dimension named above; each array names one. Nothing has to cross between parts.
Inputs may be any that keep to these rules, and one draw needn't show every extreme that they name: `vertical`: each row holds 8 different key-block numbers, block 0 and block 63 among them. `slash_offsets`: each row holds 8 different block offsets, offset 0 and offset 64 - 1 among them.
All inputs are finite; a program needn't handle non-finite values.
Results may differ from the reference program's by a relative error of at most 0.006.
Values may be sent and summed in bfloat16 or wider, within the bound.
A program may use at most 64 MiB of HBM per device.

```python
import math
import jax
import jax.numpy as jnp
from jax import lax

H = 8
HD = 128
BLK = 64
NV = 8
NS = 8
SEQ = 4096
NB = 64


def paired_draw(base_key):
    query_key = jax.random.fold_in(base_key, 101)
    key_key = jax.random.fold_in(base_key, 102)
    key_values = jnp.clip(jax.random.normal(key_key, (SEQ, HD), jnp.float32), -6.0, 6.0)
    query_values = jnp.clip(jax.random.normal(query_key, (SEQ, H * HD), jnp.float32), -6.0, 6.0)
    return (query_values, key_values)


def draw_queries(key, part):
    return paired_draw(key)[0].astype(jnp.bfloat16)


def draw_key_rows(key, part):
    return paired_draw(key)[1].astype(jnp.bfloat16)


def draw_vertical(key, part):

    def head_blocks(head_key):
        others = jax.random.permutation(head_key, NB - 2)[:NV - 2].astype(jnp.int32) + 1
        first = jnp.zeros((1,), jnp.int32)
        last = jnp.full((1,), NB - 1, jnp.int32)
        return jnp.concatenate([first, others, last])
    return jax.vmap(head_blocks)(jax.random.split(jax.random.fold_in(key, 201), H))


def draw_slash_offsets(key, part):

    def head_offsets(head_key):
        near_key = jax.random.fold_in(head_key, 1)
        far_key = jax.random.fold_in(head_key, 2)
        nearby = jax.random.permutation(near_key, 2 * NS)[:NS // 2 - 1].astype(jnp.int32) + 1
        distant = jax.random.permutation(far_key, NB - 2 * NS - 2)[:NS // 2 - 1].astype(jnp.int32) + 2 * NS + 1
        last = jnp.full((1,), NB - 1, jnp.int32)
        return jnp.concatenate([jnp.zeros((1,), jnp.int32), nearby, distant, last])
    return jax.vmap(head_offsets)(jax.random.split(jax.random.fold_in(key, 301), H))


def shard_levels(key, dims, shards, smallest, high):
    factor_of, own = 1.0, jax.random.fold_in(key, 6)
    for dim, blocks in shards:
        heights = jnp.exp(jax.random.uniform(jax.random.fold_in(own, dim), (blocks,), jnp.float32, smallest / len(shards), high / len(shards)))
        factor_of = factor_of * jnp.repeat(heights, dims[dim] // blocks).reshape([-1 if axis == dim else 1 for axis in range(len(dims))])
    return factor_of


def centred(own_key, dims, width, limit, cuts=(), held_as=jnp.bfloat16):
    array = width * jax.random.normal(own_key, dims, jnp.float32)
    if cuts:
        array = array * shard_levels(own_key, dims, cuts, -0.22, 0.18)
    return jnp.clip(array, -limit, limit).astype(held_as)


def setup_inputs(seed: int = 0, part: int = 0) -> dict:
    key_list = jax.random.split(jax.random.key(seed), 6)
    part_keys = jax.random.split(jax.random.fold_in(key_list[5], part), 6)
    return {
        "queries": draw_queries(jax.random.fold_in(jax.random.fold_in(key_list[5], part), 71), part),
        "key_rows": draw_key_rows(jax.random.fold_in(jax.random.fold_in(key_list[5], part), 71), part),
        "value_rows": centred(part_keys[2], (SEQ, HD), 1.0, 6.0, ((0, 16),)),
        "vertical": draw_vertical(jax.random.fold_in(jax.random.fold_in(key_list[5], part), 71), part),
        "slash_offsets": draw_slash_offsets(jax.random.fold_in(jax.random.fold_in(key_list[5], part), 71), part),
    }


def reference(queries, key_rows, value_rows, vertical, slash_offsets):
    block_ids = jnp.arange(NB, dtype=jnp.int32)
    vertical_hit = jnp.any(vertical[:, :, None] == block_ids[None, None, :], axis=1)
    slash_hit = jnp.any(slash_offsets[:, :, None] == block_ids[None, None, :], axis=1)
    block_gap = block_ids[:, None] - block_ids[None, :]
    slash_at = jnp.take(slash_hit, jnp.clip(block_gap, 0, NB - 1), axis=1)
    live_blocks = (block_gap >= 0)[None] & (vertical_hit[:, None, :] | slash_at)
    row_count = 4 * BLK
    scale_factor = 1.0 / math.sqrt(HD)
    keys_wide = key_rows.astype(jnp.float32)
    values_wide = value_rows.astype(jnp.float32)
    positions = jnp.arange(SEQ, dtype=jnp.int32)

    def attend_rows(block_number):
        row_start = (block_number * row_count).astype(jnp.int32)
        query_part = lax.dynamic_slice_in_dim(queries, row_start, row_count, 0).astype(jnp.float32)
        query_part = query_part.reshape(row_count, H, HD)
        scores = jnp.einsum('rhd,kd->hrk', query_part, keys_wide) * scale_factor
        block_live = lax.dynamic_slice_in_dim(live_blocks, (block_number * 4).astype(jnp.int32), 4, 1)
        token_live = jnp.repeat(jnp.repeat(block_live, BLK, axis=1), BLK, axis=2)
        query_positions = row_start + jnp.arange(row_count, dtype=jnp.int32)
        allowed = token_live & (positions[None, :] <= query_positions[:, None])[None]
        row_max = lax.optimization_barrier(jnp.max(jnp.where(allowed, scores, -jnp.inf), axis=-1, keepdims=True))
        weights = jnp.where(allowed, jnp.exp(scores - row_max), 0.0)
        total = lax.optimization_barrier(jnp.sum(weights, axis=-1))
        rounded = lax.optimization_barrier(weights.astype(jnp.bfloat16)).astype(jnp.float32)
        mixed_sum = jnp.einsum('hrk,kd->hrd', rounded, values_wide)
        result = mixed_sum / total[..., None]
        return result.transpose(1, 0, 2).reshape(row_count, H * HD).astype(jnp.bfloat16)
    blocks_out = lax.map(attend_rows, jnp.arange(SEQ // row_count, dtype=jnp.int32))
    return blocks_out.reshape(SEQ, H * HD)
```

```python
import functools
import math

import jax
import jax.numpy as jnp
from jax import lax
from jax.experimental import pallas as pl
from jax.experimental.pallas import tpu as pltpu
from jax.sharding import PartitionSpec as P

BLK = 64
DEAD = -1e30
MESH = pl.DeviceIdType.MESH


def relay(sizes, k_hbm, v_hbm, kv, local_sem, zs, zr, ys, yr, cs, cr):
    Z, W, C = sizes
    R = k_hbm.shape[0]
    part = lax.axis_index("parts")
    outer = lax.axis_index("outer")
    c = lax.axis_index("inner")
    z, y = outer // W, outer % W

    def rows(zz, yy, cc):
        return pl.ds(pl.multiple_of(((zz * W + yy) * C + cc) * R, R), R)

    loads = [
        pltpu.make_async_copy(k_hbm, kv.at[0, rows(z, y, c)], local_sem.at[0]),
        pltpu.make_async_copy(v_hbm, kv.at[1, rows(z, y, c)], local_sem.at[1]),
    ]
    for load in loads:
        load.start()

    up = (part, (z + 1) * W + y, c)
    down = (part, (z - 1) * W + y, c)
    across = (part, z * W + (1 - y), c)
    twin = (part, outer, 1 - c)

    barrier = pltpu.get_barrier_semaphore()

    def greet(who):
        pl.semaphore_signal(barrier, inc=1, device_id=who, device_id_type=MESH)

    greet(twin)
    if W == 2:
        greet(across)

    @pl.when(z > 0)
    def _():
        greet(down)

    @pl.when(z < Z - 1)
    def _():
        greet(up)

    pl.semaphore_wait(
        barrier, W + jnp.where(z > 0, 1, 0) + jnp.where(z < Z - 1, 1, 0)
    )

    def copy(t, where, who, send, recv, own=False):
        return pltpu.make_async_remote_copy(
            src_ref=(k_hbm, v_hbm)[t] if own else kv.at[t, where], dst_ref=kv.at[t, where],
            send_sem=send, recv_sem=recv, device_id=who, device_id_type=MESH,
        )

    def z_copy(t, zz, own=False):
        return copy(t, rows(zz, y, c), up, zs.at[t, zz], zr.at[t, zz], own)

    def y_copy(t, zz, yy, own=False):
        return copy(t, rows(zz, yy, c), across, ys.at[t, zz], yr.at[t, zz], own)

    def c_copy(t, zz, yy, cc, own=False):
        return copy(t, rows(zz, yy, cc), twin, cs.at[t, yy, zz], cr.at[t, yy, zz], own)

    def send_shard(t, zz, own):
        @pl.when(z < Z - 1)
        def _():
            z_copy(t, zz, own).start()

        if W == 2:
            if own:
                @pl.when(y == 0)
                def _():
                    y_copy(t, zz, y, True).start()
            else:
                y_copy(t, zz, y).start()
        if own:
            @pl.when(c == 0)
            def _():
                c_copy(t, zz, y, c, True).start()
        else:
            c_copy(t, zz, y, c).start()

    for t in range(2):
        send_shard(t, z, True)

    def relay_across(zz):
        for t in range(2):
            y_copy(t, zz, 1 - y).wait_recv()
            c_copy(t, zz, 1 - y, c).start()

    def step(j, carry):
        zz = z - j
        for t in range(2):
            z_copy(t, zz).wait_recv()
            send_shard(t, zz, False)
        if W == 2:
            @pl.when((j > 1) | (y == 1))
            def _():
                relay_across(zz + 1)
        return carry

    lax.fori_loop(1, z + 1, step, 0)
    if W == 2:
        @pl.when((z > 0) | (y == 1))
        def _():
            relay_across(0)

    def arrivals(zz, carry):
        for t in range(2):
            c_copy(t, zz, y, 1 - c).wait_recv()
            if W == 2:
                c_copy(t, zz, 1 - y, 1 - c).wait_recv()
        return carry

    def sends(zz, carry):
        for t in range(2):
            c_copy(t, zz, y, c).wait_send()
            if W == 2:
                c_copy(t, zz, 1 - y, c).wait_send()
                y_copy(t, zz, y).wait_send()
        return carry

    def z_sends(zz, carry):
        for t in range(2):
            z_copy(t, zz).wait_send()
        return carry

    lax.fori_loop(0, z, arrivals, 0)
    for t in range(2):
        @pl.when(c == 1)
        def _():
            c_copy(t, z, y, 1 - c).wait_recv()

        if W == 2:
            @pl.when(y == 1)
            def _():
                c_copy(t, z, 1 - y, 1 - c).wait_recv()

    for load in loads:
        load.wait()
    lax.fori_loop(0, z, sends, 0)
    for t in range(2):
        @pl.when(c == 0)
        def _():
            c_copy(t, z, y, c).wait_send()

        if W == 2:
            @pl.when(y == 1)
            def _():
                c_copy(t, z, 1 - y, c).wait_send()

            @pl.when(y == 0)
            def _():
                y_copy(t, z, y).wait_send()

    @pl.when(z < Z - 1)
    def _():
        lax.fori_loop(0, z + 1, z_sends, 0)


def attend(vert, slash, q_ref, kv, out, kb_tab, bias_tab):
    heads, nv = vert.shape
    ns = slash.shape[1]
    R = q_ref.shape[0]
    hd = kv.shape[2]
    QB = R // BLK
    NB = kv.shape[1] // BLK
    own_block = (lax.axis_index("outer") * lax.axis_size("inner") + lax.axis_index("inner")) * QB

    def tables(h, carry):
        def compact(ref, n, end):
            vals = [ref[h, s] for s in range(n)]
            drop = [(v == end[0]) | (v == end[1]) for v in vals]
            first = jnp.where(drop[n - 2], vals[n - 1], vals[n - 2])
            res, used = [], None
            for s in range(n - 2):
                if used is None:
                    fill = first
                    used = drop[s]
                else:
                    fill = jnp.where(used, vals[n - 1], first)
                    used = used | drop[s]
                res.append(jnp.where(drop[s], fill, vals[s]))
            return res

        offsets = compact(slash, ns, (0, NB - 1))
        columns = [jnp.int32(0)] + compact(vert, nv, (0, NB - 1))
        for b in range(QB):
            i = own_block + b
            slot = 0
            for o in offsets:
                kb = i - o
                dead = kb < 0
                for col in columns:
                    dead = dead | (kb == col)
                kb_tab[h, b * 16 + slot] = jnp.where(dead, 0, kb)
                bias_tab[h, b * 16 + slot] = jnp.where(dead, DEAD, 0.0).astype(jnp.float32)
                slot += 1
            for col in columns:
                dead = col >= i
                kb_tab[h, b * 16 + slot] = jnp.where(dead, 0, col)
                bias_tab[h, b * 16 + slot] = jnp.where(dead, DEAD, 0.0).astype(jnp.float32)
                slot += 1
        return carry

    lax.fori_loop(0, heads, tables, 0)

    factor = math.log2(math.e) / math.sqrt(hd)
    lane = lax.broadcasted_iota(jnp.int32, (BLK, 2 * BLK), 1)
    row = lax.broadcasted_iota(jnp.int32, (BLK, 2 * BLK), 0)
    left = lane < BLK
    above = left & (lane > row)

    def one_head(h, carry):
        cols = pl.ds(pl.multiple_of(h * hd, hd), hd)
        for b in range(QB):
            q = q_ref[b * BLK:(b + 1) * BLK, cols]
            slots = ns - 2 + nv - 1
            kbs = [own_block + b] + [kb_tab[h, b * 16 + s] for s in range(slots)]
            bias = [None] + [bias_tab[h, b * 16 + s] for s in range(slots)]
            starts = [pl.multiple_of(kb * BLK, BLK) for kb in kbs]
            keys = jnp.concatenate([kv[0, pl.ds(s, BLK), :] for s in starts], axis=0)
            values = jnp.concatenate([kv[1, pl.ds(s, BLK), :] for s in starts], axis=0)
            scores = lax.dot_general(
                q, keys, (((1,), (1,)), ((), ())), preferred_element_type=jnp.float32
            )
            tiles = []
            for g in range(len(kbs) // 2):
                if g == 0:
                    shift = jnp.where(above, DEAD, jnp.where(left, 0.0, bias[1]))
                else:
                    shift = jnp.where(left, bias[2 * g], bias[2 * g + 1])
                tiles.append(scores[:, g * 2 * BLK:(g + 1) * 2 * BLK] * factor + shift)
            top = functools.reduce(jnp.maximum, tiles)
            top = jnp.max(top, axis=1, keepdims=True)
            weights = [jnp.exp2(t - top) for t in tiles]
            total = jnp.sum(functools.reduce(jnp.add, weights), axis=1, keepdims=True)
            rounded = jnp.concatenate([w.astype(jnp.bfloat16) for w in weights], axis=1)
            mixed = jnp.dot(rounded, values, preferred_element_type=jnp.float32)
            out[b * BLK:(b + 1) * BLK, cols] = (mixed * (1.0 / total)).astype(out.dtype)
        return carry

    lax.fori_loop(0, heads, one_head, 0)


def shards(sizes, queries, key_rows, value_rows, vertical, slash_offsets):
    Z, W, C = sizes
    R, hd = key_rows.shape
    heads = vertical.shape[0]
    dma = pltpu.SemaphoreType.DMA
    kv = pl.pallas_call(
        functools.partial(relay, sizes),
        out_shape=jax.ShapeDtypeStruct((2, Z * W * C * R, hd), jnp.bfloat16),
        in_specs=[pl.BlockSpec(memory_space=pltpu.HBM)] * 2,
        out_specs=pl.BlockSpec(memory_space=pl.ANY),
        scratch_shapes=[
            dma((2,)),
            dma((2, Z)), dma((2, Z)),
            dma((2, Z)), dma((2, Z)),
            dma((2, W, Z)), dma((2, W, Z)),
        ],
        compiler_params=pltpu.CompilerParams(
            collective_id=0, has_side_effects=True, vmem_limit_bytes=1 << 20
        ),
    )(key_rows, value_rows)
    smem = pl.BlockSpec(memory_space=pltpu.SMEM)
    vmem = pl.BlockSpec(memory_space=pltpu.VMEM)
    return pl.pallas_call(
        attend,
        out_shape=jax.ShapeDtypeStruct(queries.shape, jnp.bfloat16),
        in_specs=[smem, smem, vmem, vmem],
        out_specs=vmem,
        scratch_shapes=[
            pltpu.SMEM((heads, 16 * (R // BLK)), jnp.int32),
            pltpu.SMEM((heads, 16 * (R // BLK)), jnp.float32),
        ],
        compiler_params=pltpu.CompilerParams(vmem_limit_bytes=32 << 20),
    )(vertical, slash_offsets, queries, kv)


def solution(mesh):
    outer = mesh.shape["outer"]
    columns = 2 if len(mesh.devices) <= 2 and outer % 2 == 0 else 1
    sizes = (outer // columns, columns, mesh.shape["inner"])
    rows = P(("parts", "outer", "inner"), None)
    in_specs = (rows, rows, rows, P("parts", None), P("parts", None))
    return jax.shard_map(
        functools.partial(shards, sizes), mesh=mesh, in_specs=in_specs, out_specs=rows,
        check_vma=False,
    )
```

```python
import functools
import math

import jax
import jax.numpy as jnp
from jax import lax
from jax.experimental import pallas as pl
from jax.experimental.pallas import tpu as pltpu
from jax.sharding import PartitionSpec as P

BLK = 64
DEAD = -1e30
UNROLL = 4
MESH = pl.DeviceIdType.MESH


def relay(sizes, k_hbm, v_hbm, kv, local_sem, zs, zr, ys, yr, cs, cr):
    Z, W, C = sizes
    R = k_hbm.shape[0]
    part = lax.axis_index("parts")
    outer = lax.axis_index("outer")
    c = lax.axis_index("inner")
    z, y = outer // W, outer % W

    def rows(zz, yy, cc):
        return pl.ds(pl.multiple_of(((zz * W + yy) * C + cc) * R, R), R)

    loads = [
        pltpu.make_async_copy(k_hbm, kv.at[0, rows(z, y, c)], local_sem.at[0]),
        pltpu.make_async_copy(v_hbm, kv.at[1, rows(z, y, c)], local_sem.at[1]),
    ]
    for load in loads:
        load.start()

    up = (part, (z + 1) * W + y, c)
    down = (part, (z - 1) * W + y, c)
    across = (part, z * W + (1 - y), c)
    twin = (part, outer, 1 - c)

    barrier = pltpu.get_barrier_semaphore()

    def greet(who):
        pl.semaphore_signal(barrier, inc=1, device_id=who, device_id_type=MESH)

    greet(twin)
    if W == 2:
        greet(across)

    @pl.when(z > 0)
    def _():
        greet(down)

    @pl.when(z < Z - 1)
    def _():
        greet(up)

    pl.semaphore_wait(
        barrier, W + jnp.where(z > 0, 1, 0) + jnp.where(z < Z - 1, 1, 0)
    )

    def copy(t, where, who, send, recv, own=False):
        return pltpu.make_async_remote_copy(
            src_ref=(k_hbm, v_hbm)[t] if own else kv.at[t, where], dst_ref=kv.at[t, where],
            send_sem=send, recv_sem=recv, device_id=who, device_id_type=MESH,
        )

    def z_copy(t, zz, own=False):
        return copy(t, rows(zz, y, c), up, zs.at[t, zz], zr.at[t, zz], own)

    def y_copy(t, zz, yy, own=False):
        return copy(t, rows(zz, yy, c), across, ys.at[t, zz], yr.at[t, zz], own)

    def c_copy(t, zz, yy, cc, own=False):
        return copy(t, rows(zz, yy, cc), twin, cs.at[t, yy, zz], cr.at[t, yy, zz], own)

    def send_shard(t, zz, own):
        @pl.when(z < Z - 1)
        def _():
            z_copy(t, zz, own).start()

        if W == 2:
            if own:
                @pl.when(y == 0)
                def _():
                    y_copy(t, zz, y, True).start()
            else:
                y_copy(t, zz, y).start()
        if own:
            @pl.when(c == 0)
            def _():
                c_copy(t, zz, y, c, True).start()
        else:
            c_copy(t, zz, y, c).start()

    for t in range(2):
        send_shard(t, z, True)

    def relay_across(zz):
        for t in range(2):
            y_copy(t, zz, 1 - y).wait_recv()
            c_copy(t, zz, 1 - y, c).start()

    def step(j, carry):
        zz = z - j
        for t in range(2):
            z_copy(t, zz).wait_recv()
            send_shard(t, zz, False)
        if W == 2:
            @pl.when((j > 1) | (y == 1))
            def _():
                relay_across(zz + 1)
        return carry

    lax.fori_loop(1, z + 1, step, 0)
    if W == 2:
        @pl.when((z > 0) | (y == 1))
        def _():
            relay_across(0)

    def arrivals(zz, carry):
        for t in range(2):
            c_copy(t, zz, y, 1 - c).wait_recv()
            if W == 2:
                c_copy(t, zz, 1 - y, 1 - c).wait_recv()
        return carry

    def sends(zz, carry):
        for t in range(2):
            c_copy(t, zz, y, c).wait_send()
            if W == 2:
                c_copy(t, zz, 1 - y, c).wait_send()
                y_copy(t, zz, y).wait_send()
        return carry

    def z_sends(zz, carry):
        for t in range(2):
            z_copy(t, zz).wait_send()
        return carry

    lax.fori_loop(0, z, arrivals, 0)
    for t in range(2):
        @pl.when(c == 1)
        def _():
            c_copy(t, z, y, 1 - c).wait_recv()

        if W == 2:
            @pl.when(y == 1)
            def _():
                c_copy(t, z, 1 - y, 1 - c).wait_recv()

    for load in loads:
        load.wait()
    lax.fori_loop(0, z, sends, 0)
    for t in range(2):
        @pl.when(c == 0)
        def _():
            c_copy(t, z, y, c).wait_send()

        if W == 2:
            @pl.when(y == 1)
            def _():
                c_copy(t, z, 1 - y, c).wait_send()

            @pl.when(y == 0)
            def _():
                y_copy(t, z, y).wait_send()

    @pl.when(z < Z - 1)
    def _():
        lax.fori_loop(0, z + 1, z_sends, 0)


def attend(vert, slash, q_ref, kv, out, marks):
    heads, nv = vert.shape
    ns = slash.shape[1]
    R = q_ref.shape[0]
    hd = kv.shape[2]
    QB = R // BLK
    NB = kv.shape[1] // BLK
    own_block = (lax.axis_index("outer") * lax.axis_size("inner") + lax.axis_index("inner")) * QB

    def clear(n, carry):
        for u in range(8):
            marks[n * 8 + u] = -1
        return carry

    lax.fori_loop(0, NB // 8, clear, 0)

    factor = math.log2(math.e) / math.sqrt(hd)
    lane = lax.broadcasted_iota(jnp.int32, (BLK, 2 * BLK), 1)
    row = lax.broadcasted_iota(jnp.int32, (BLK, 2 * BLK), 0)
    left = lane < BLK
    above = left & (lane > row)
    nt = (((1,), (1,)), ((), ()))

    def compact(ref, h, n):
        vals = [ref[h, s] for s in range(n)]
        drop = [(v == 0) | (v == NB - 1) for v in vals]
        fill = jnp.where(drop[n - 2], vals[n - 1], vals[n - 2])
        kept = []
        for s in range(n - 2):
            kept.append(jnp.where(drop[s], fill, vals[s]))
            fill = jnp.where(drop[s], vals[n - 1], fill)
        return kept

    def gather(t, blocks):
        return jnp.concatenate(
            [kv[t, pl.ds(pl.multiple_of(kb * BLK, BLK), BLK), :] for kb in blocks], axis=0
        )

    def dead_bias(dead):
        return jnp.where(dead, DEAD, 0.0).astype(jnp.float32)

    def one_head(h):
        cols = pl.ds(pl.multiple_of(h * hd, hd), hd)
        columns = compact(vert, h, nv)
        offsets = compact(slash, h, ns)
        for col in columns:
            marks[col] = h
        shared = [jnp.minimum(col, own_block + QB - 1) for col in columns]
        shared_scores = lax.dot_general(
            q_ref[:, cols], gather(0, shared), nt, preferred_element_type=jnp.float32
        )
        shared_values = gather(1, shared)
        groups = len(columns) // 2
        shared_weights, own = [], []
        for b in range(QB):
            i = own_block + b
            at = slice(b * BLK, (b + 1) * BLK)
            kbs, bias = [i, jnp.int32(0)], [None, dead_bias(i == 0)]
            for o in offsets:
                kb = jnp.maximum(i - o, 0)
                kbs.append(kb)
                bias.append(dead_bias((i <= o) | (marks[kb] == h)))
            scores = lax.dot_general(
                q_ref[at, cols], gather(0, kbs), nt, preferred_element_type=jnp.float32
            )
            tiles = []
            for g in range(groups):
                d0, d1 = dead_bias(columns[2 * g] >= i), dead_bias(columns[2 * g + 1] >= i)
                shift = jnp.where(left, d0, d1)
                tiles.append(shared_scores[at, g * 2 * BLK:(g + 1) * 2 * BLK] * factor + shift)
            for g in range(len(kbs) // 2):
                if g == 0:
                    shift = jnp.where(above, DEAD, jnp.where(left, 0.0, bias[1]))
                else:
                    shift = jnp.where(left, bias[2 * g], bias[2 * g + 1])
                tiles.append(scores[:, g * 2 * BLK:(g + 1) * 2 * BLK] * factor + shift)
            top = jnp.max(functools.reduce(jnp.maximum, tiles), axis=1, keepdims=True)
            weights = [jnp.exp2(t - top) for t in tiles]
            total = jnp.sum(functools.reduce(jnp.add, weights), axis=1, keepdims=True)
            rounded = [w.astype(jnp.bfloat16) for w in weights]
            shared_weights.append(jnp.concatenate(rounded[:groups], axis=1))
            mixed = jnp.dot(
                jnp.concatenate(rounded[groups:], axis=1), gather(1, kbs),
                preferred_element_type=jnp.float32,
            )
            own.append((at, mixed, total))
        shared_mixed = jnp.dot(
            jnp.concatenate(shared_weights, axis=0), shared_values,
            preferred_element_type=jnp.float32,
        )
        for at, mixed, total in own:
            out[at, cols] = ((mixed + shared_mixed[at, :]) * (1.0 / total)).astype(out.dtype)

    def some_heads(n, carry):
        for u in range(UNROLL):
            one_head(n * UNROLL + u)
        return carry

    lax.fori_loop(0, heads // UNROLL, some_heads, 0)


def shards(sizes, queries, key_rows, value_rows, vertical, slash_offsets):
    Z, W, C = sizes
    R, hd = key_rows.shape
    dma = pltpu.SemaphoreType.DMA
    key_rows = pltpu.with_memory_space_constraint(key_rows, pltpu.HBM)
    value_rows = pltpu.with_memory_space_constraint(value_rows, pltpu.HBM)
    kv = pl.pallas_call(
        functools.partial(relay, sizes),
        out_shape=jax.ShapeDtypeStruct((2, Z * W * C * R, hd), jnp.bfloat16),
        in_specs=[pl.BlockSpec(memory_space=pltpu.HBM)] * 2,
        out_specs=pl.BlockSpec(memory_space=pl.ANY),
        scratch_shapes=[
            dma((2,)),
            dma((2, Z)), dma((2, Z)),
            dma((2, Z)), dma((2, Z)),
            dma((2, W, Z)), dma((2, W, Z)),
        ],
        compiler_params=pltpu.CompilerParams(
            collective_id=0, has_side_effects=True, vmem_limit_bytes=1 << 20
        ),
    )(key_rows, value_rows)
    smem = pl.BlockSpec(memory_space=pltpu.SMEM)
    vmem = pl.BlockSpec(memory_space=pltpu.VMEM)
    return pl.pallas_call(
        attend,
        out_shape=jax.ShapeDtypeStruct(queries.shape, jnp.bfloat16),
        in_specs=[smem, smem, vmem, vmem],
        out_specs=vmem,
        scratch_shapes=[
            pltpu.SMEM((Z * W * C * R // BLK,), jnp.int32),
        ],
        compiler_params=pltpu.CompilerParams(vmem_limit_bytes=32 << 20),
    )(vertical, slash_offsets, queries, kv)


def solution(mesh):
    outer = mesh.shape["outer"]
    columns = 2 if len(mesh.devices) <= 2 and outer % 2 == 0 else 1
    sizes = (outer // columns, columns, mesh.shape["inner"])
    rows = P(("parts", "outer", "inner"), None)
    in_specs = (rows, rows, rows, P("parts", None), P("parts", None))
    return jax.shard_map(
        functools.partial(shards, sizes), mesh=mesh, in_specs=in_specs, out_specs=rows,
        check_vma=False,
    )
```
